256 devices in a mesh: feeder: 64 (over z, x, core), node: 4 (over y).
Axes of the slice: x: 4, y: 4, z: 8, core: 2. Of those that a mesh axis runs over, the one named last changes fastest.
Arguments:
- factors: bfloat16 [2048, 256], P('node'), may hold values from -6 to 6
- loadings: bfloat16 [32768, 256], P(('feeder', 'node')), may hold values from -0.35355339 to 0.5
- parents: int32 [32768], P(('feeder', 'node')), may hold values from -1 to 126, as said below
- load_base: float32 [2, 32768], P(None, ('feeder', 'node')), may hold values from 2.4414063e-06 to 0.00048828125, as said below
- lateral_z: float32 [2, 32768], P(None, ('feeder', 'node')), may hold values from 0.007 to 0.175, as said below
- trunk_z: float32 [2, 64, 4], P(None, 'feeder', 'node'), may hold values from 0.00034375 to 0.00609375, as said below
Outputs:
- volt_real: float32 [2048, 32768], P(None, ('feeder', 'node'))
- volt_imag: float32 [2048, 32768], P(None, ('feeder', 'node'))
The draws below stay inside these ranges and needn't reach their ends.
Inputs may be any that keep to these rules, and one draw needn't show every extreme that they name: `parents`: within each aligned run of 128 nodes (one lateral), a node's entry is the position of its parent in the same lateral, which comes before it, or -1 for a branch from the section's head node; the first node of every lateral has -1 and the last node's parent is the node just before it. `load_base`: with unit = 1 / 8192, row 0 lies between 1 and 4 units and row 1 between 0.02 and 0.08 units. `lateral_z`: with unit = 128 * 64 / 128^2, row 0 lies between 0.014 and 0.056 units and row 1 between 0.087 and 0.35 units. `trunk_z`: with unit = 1 / 64, row 0 lies between 0.022 and 0.066 units and row 1 between 0.13 and 0.39 units.
All inputs are finite; a program needn't handle non-finite values.
Results may differ from the reference program's by a relative error of at most 0.0003.
Values may be sent and summed in bfloat16 or wider, within the bound.
A program may use at most 64 MiB of HBM per device.

```python
import jax
import jax.numpy as jnp
from jax import lax

R = 256
LAT_NODES = 128
LAT_DEV = 1
SCEN = 2048
SWEEPS = 3
NODES_DEV = 128
SECTIONS = 64
CIRCUITS = 4
NODES = 32768


def draw_factors(key, part):
    common = jax.random.uniform(jax.random.fold_in(key, 61), (SCEN, 1), jnp.float32, -6.0, 6.0)
    others = jnp.clip(jax.random.normal(jax.random.fold_in(key, 67), (SCEN, R - 1), jnp.float32), -6.0, 6.0)
    return jnp.concatenate([common, others], axis=1).astype(jnp.bfloat16)


def draw_loadings(key, part):
    spread = (R // 2) ** (-0.5)
    common = jax.random.uniform(jax.random.fold_in(key, 71), (NODES, 1), jnp.float32, 0.3, 0.5)
    others = spread * jnp.clip(jax.random.normal(jax.random.fold_in(key, 73), (NODES, R - 1), jnp.float32), -4.0, 4.0)
    return jnp.concatenate([common, others], axis=1).astype(jnp.bfloat16)


def draw_parents(key, part):
    position = jnp.arange(NODES, dtype=jnp.int32) % LAT_NODES
    stride = jax.random.randint(jax.random.fold_in(key, 17), (NODES,), 1, 5, dtype=jnp.int32)
    parent_pos = position - stride
    parent_pos = jnp.where(parent_pos < -1, -1, parent_pos)
    parent_pos = jnp.where(position == 0, -1, parent_pos)
    parent_pos = jnp.where(position == LAT_NODES - 1, LAT_NODES - 2, parent_pos)
    return parent_pos.astype(jnp.int32)


def log_between(key, shape, low, high):
    unit_draw = jax.random.uniform(key, shape, jnp.float32)
    return low * jnp.exp(unit_draw * jnp.log(high / low))


def draw_load_base(key, part):
    scale = 1.0 / (NODES_DEV * SECTIONS)
    active = log_between(jax.random.fold_in(key, 31), (NODES,), scale, 4.0 * scale)
    reactive = log_between(jax.random.fold_in(key, 37), (NODES,), 0.02 * scale, 0.08 * scale)
    return jnp.stack([active, reactive]).astype(jnp.float32)


def draw_lateral_z(key, part):
    scale = NODES_DEV * SECTIONS / (LAT_NODES * LAT_NODES)
    resist = log_between(jax.random.fold_in(key, 41), (NODES,), 0.014 * scale, 0.056 * scale)
    react = log_between(jax.random.fold_in(key, 43), (NODES,), 0.087 * scale, 0.35 * scale)
    return jnp.stack([resist, react]).astype(jnp.float32)


def draw_trunk_z(key, part):
    scale = 1.0 / SECTIONS
    resist = log_between(jax.random.fold_in(key, 47), (SECTIONS, CIRCUITS), 0.022 * scale, 0.066 * scale)
    react = log_between(jax.random.fold_in(key, 53), (SECTIONS, CIRCUITS), 0.13 * scale, 0.39 * scale)
    return jnp.stack([resist, react]).astype(jnp.float32)


def setup_inputs(seed: int = 0) -> dict:
    key_of = jax.random.split(jax.random.key(seed), 7)
    factors = draw_factors(jax.random.fold_in(key_of[6], 71), 0)
    loadings = draw_loadings(jax.random.fold_in(key_of[6], 71), 0)
    parents = draw_parents(jax.random.fold_in(key_of[6], 71), 0)
    load_base = draw_load_base(jax.random.fold_in(key_of[6], 71), 0)
    lateral_z = draw_lateral_z(jax.random.fold_in(key_of[6], 71), 0)
    trunk_z = draw_trunk_z(jax.random.fold_in(key_of[6], 71), 0)
    return {"factors": factors, "loadings": loadings, "parents": parents, "load_base": load_base, "lateral_z": lateral_z, "trunk_z": trunk_z}


HIGHEST = lax.Precision.HIGHEST


def path_matrix(parent_rows):
    laterals, width = parent_rows.shape
    column = jnp.arange(width, dtype=jnp.int32)
    adjacency = (parent_rows[:, :, None] == column[None, None, :]).astype(jnp.float32)
    identity = jnp.eye(width, dtype=jnp.float32)
    paths = identity[None] + adjacency
    power = adjacency
    for turn in range((width - 1).bit_length() - 1):
        power = jnp.einsum("alm,amn->aln", power, power, precision=HIGHEST)
        paths = paths + jnp.einsum("alm,amn->aln", paths, power, precision=HIGHEST)
    return paths


def node_currents(active, reactive, real_part, imag_part):
    magnitude = real_part * real_part + imag_part * imag_part
    return (active * real_part + reactive * imag_part) / magnitude, (active * imag_part - reactive * real_part) / magnitude


def reference(factors, loadings, parents, load_base, lateral_z, trunk_z):
    level = jnp.dot(factors, loadings.T, preferred_element_type=jnp.float32).astype(jnp.bfloat16)
    width = NODES_DEV * CIRCUITS
    scen = factors.shape[0]
    lat_count = CIRCUITS * LAT_DEV
    section_data = []
    for section_index in range(SECTIONS):
        lower = section_index * width
        swing = 1.0 + 0.5 * jnp.tanh(level[:, lower:lower + width].astype(jnp.float32))
        active = load_base[0, lower:lower + width][None, :] * swing
        reactive = load_base[1, lower:lower + width][None, :] * swing
        paths = path_matrix(parents[lower:lower + width].reshape(lat_count, LAT_NODES))
        resist = lateral_z[0, lower:lower + width].reshape(lat_count, LAT_NODES)
        react = lateral_z[1, lower:lower + width].reshape(lat_count, LAT_NODES)
        section_data.append((active, reactive, paths, resist, react))
    volts = [(jnp.ones((scen, width), jnp.float32), jnp.zeros((scen, width), jnp.float32)) for section_index in range(SECTIONS)]
    for sweep_index in range(SWEEPS):
        currents = []
        inject_real = []
        inject_imag = []
        for section_index in range(SECTIONS):
            active, reactive, paths, resist, react = section_data[section_index]
            current_real, current_imag = node_currents(active, reactive, volts[section_index][0], volts[section_index][1])
            currents.append((current_real, current_imag))
            inject_real.append(jnp.sum(current_real.reshape(scen, CIRCUITS, NODES_DEV), axis=2))
            inject_imag.append(jnp.sum(current_imag.reshape(scen, CIRCUITS, NODES_DEV), axis=2))
        inject_real = jnp.stack(inject_real)
        inject_imag = jnp.stack(inject_imag)
        trunk_real = jnp.flip(jnp.cumsum(jnp.flip(inject_real, 0), 0), 0)
        trunk_imag = jnp.flip(jnp.cumsum(jnp.flip(inject_imag, 0), 0), 0)
        resist_trunk = trunk_z[0][:, None, :]
        react_trunk = trunk_z[1][:, None, :]
        drop_real = resist_trunk * trunk_real - react_trunk * trunk_imag
        drop_imag = resist_trunk * trunk_imag + react_trunk * trunk_real
        head_real = 1.0 - jnp.cumsum(drop_real, 0)
        head_imag = -jnp.cumsum(drop_imag, 0)
        new_volts = []
        for section_index in range(SECTIONS):
            active, reactive, paths, resist, react = section_data[section_index]
            current_real, current_imag = currents[section_index]
            stacked = jnp.stack([current_real, current_imag]).reshape(2, scen, lat_count, LAT_NODES)
            branch = jnp.einsum("csal,alm->csam", stacked, paths, precision=HIGHEST)
            weighted = jnp.stack([resist * branch[0] - react * branch[1], resist * branch[1] + react * branch[0]])
            drops = jnp.einsum("csam,alm->csal", weighted, paths, precision=HIGHEST).reshape(2, scen, width)
            base_real = jnp.repeat(head_real[section_index], NODES_DEV, axis=1)
            base_imag = jnp.repeat(head_imag[section_index], NODES_DEV, axis=1)
            new_volts.append((base_real - drops[0], base_imag - drops[1]))
        volts = new_volts
    volt_real = jnp.concatenate([volts[section_index][0] for section_index in range(SECTIONS)], axis=1)
    volt_imag = jnp.concatenate([volts[section_index][1] for section_index in range(SECTIONS)], axis=1)
    return volt_real, volt_imag
```

```python
import functools

import jax
import jax.numpy as jnp
from jax import lax
from jax.experimental import pallas as pl
from jax.experimental.pallas import tpu as pltpu
from jax.sharding import PartitionSpec as P

MESH = pl.DeviceIdType.MESH
F32 = jnp.float32
BF16 = jnp.bfloat16
SWEEPS = 3
LANES = 128
PASS = 4


def dot(a, b, dims=((1,), (0,))):
    return lax.dot_general(a, b, (dims, ((), ())), preferred_element_type=F32)


def halves(value):
    high = value.astype(BF16)
    return high, (value - high.astype(F32)).astype(BF16)


def turn(tile):
    return pltpu.roll(tile, 4, 0)


def cmul(ratio, tile):
    return ratio[0] * tile + ratio[1] * turn(tile)


def body(
    slabs, slab, nodes, fac_ref, load_ref, par_ref, base_ref, latz_ref, trz_ref, out_r, out_i,
    fac, swing, cur, drop, dropl, wide, wlow, wlast, pcol, qcol, one_sec, two_sec, two_src, two_own,
    zsec, zlow, zmin, ztot, zpre, prep,
    load_v, par_v, base_v, latz_v,
    local_sem, fac_send, fac_recv, pair_send, pair_recv, zs_send, zs_recv, zt_send, zt_recv,
    one_send, one_recv, two_send, two_recv,
):
    feeder = lax.axis_index("feeder")
    node = lax.axis_index("node")
    zz = feeder // slab
    ss = lax.rem(feeder, slab)
    core = lax.rem(feeder, 2)
    partner = feeder + 1 - 2 * core
    chunk = fac.shape[1]
    half = chunk // 2
    offsets = [0, 1, nodes - 1] + [o for o in range(2, nodes - 1)]

    def slab_mate(turn_):
        return lax.rem(ss + turn_, slab)

    def at_slab(mate):
        return {"feeder": zz * slab + mate, "node": node}

    def at_other(other):
        return {"feeder": other * slab + ss, "node": node}

    def at_node(offset):
        return {"feeder": feeder, "node": lax.rem(node + offset, nodes)}

    far = sorted(range(1, slabs), key=lambda d: -min(d, slabs - d))
    wide_turns = sorted(range(1, slab), key=lambda d: -min(d, slab - d))

    barrier = pltpu.get_barrier_semaphore()
    greeted = 0
    for d in far:
        pl.semaphore_signal(barrier, inc=1, device_id=at_other(lax.rem(zz + d, slabs)), device_id_type=MESH)
        greeted += 1
    for d in wide_turns:
        pl.semaphore_signal(barrier, inc=1, device_id=at_slab(slab_mate(d)), device_id_type=MESH)
        greeted += 1
    for o in offsets[1:]:
        pl.semaphore_signal(barrier, inc=1, device_id=at_node(o), device_id_type=MESH)
        greeted += 1

    copies = [
        pltpu.make_async_copy(fac_ref, fac.at[0], local_sem.at[0]),
        pltpu.make_async_copy(load_ref, load_v, local_sem.at[1]),
        pltpu.make_async_copy(base_ref, base_v, local_sem.at[2]),
        pltpu.make_async_copy(par_ref, par_v, local_sem.at[3]),
        pltpu.make_async_copy(latz_ref, latz_v, local_sem.at[4]),
    ]
    for copy in copies:
        copy.start()
    for copy in copies:
        copy.wait()

    pcol[...] = jnp.broadcast_to(base_v[0:1, :], (LANES, LANES)).T
    qcol[...] = jnp.broadcast_to(base_v[1:2, :], (LANES, LANES)).T
    row8 = lax.broadcasted_iota(jnp.int32, (8, LANES), 0)
    upper = row8 < 4
    z_real = trz_ref[0]
    z_imag = trz_ref[1]
    zsec[ss, 0] = jnp.zeros((8, LANES), F32) + z_real
    zsec[ss, 1] = jnp.where(upper, -z_imag, z_imag)

    def level(c):
        for q in range(PASS):
            lo = q * LANES
            lev = dot(load_v[...], fac[c, lo:lo + LANES, :], ((1,), (1,)))
            swing[c, :, lo:lo + LANES] = 1.0 + 0.5 * jnp.tanh(lev.astype(BF16).astype(F32))

    rows = 16

    def currents(k, c, head):
        for q in range(PASS):
            lo = q * LANES
            if k:
                head_r = jnp.broadcast_to(head[q:q + 1, :], (rows, LANES))
                head_i = jnp.broadcast_to(head[q + 4:q + 5, :], (rows, LANES))

            def step(i, sums):
                at = pl.multiple_of(i * rows, rows)
                sw = swing[c, pl.ds(at, rows), lo:lo + LANES]
                p = pcol[pl.ds(at, rows), :]
                r = qcol[pl.ds(at, rows), :]
                if k:
                    vr = head_r - drop[c, pl.ds(at, rows), lo:lo + LANES]
                    vi = head_i - drop[c, pl.ds(LANES + at, rows), lo:lo + LANES]
                    t = sw / (vr * vr + vi * vi)
                    cr = t * (p * vr + r * vi)
                    ci = t * (p * vi - r * vr)
                else:
                    cr = sw * p
                    ci = -(sw * r)
                for part, value in ((0, cr), (1, ci)):
                    high, low = halves(value)
                    cur[c, pl.ds(part * LANES + at, rows), lo:lo + LANES] = high
                    cur[c, pl.ds((part + 2) * LANES + at, rows), lo:lo + LANES] = low
                return (
                    sums[0] + cr[0:8] + cr[8:16],
                    sums[1] + ci[0:8] + ci[8:16],
                )

            zero = jnp.zeros((8, LANES), F32)
            sum_r, sum_i = lax.fori_loop(0, LANES // rows, step, (zero, zero), unroll=4)
            one_sec[k, c, ss, q:q + 1, :] = jnp.sum(sum_r, axis=0, keepdims=True)
            one_sec[k, c, ss, q + 4:q + 5, :] = jnp.sum(sum_i, axis=0, keepdims=True)

    def send_one(k, c):
        for d in wide_turns:
            mate = slab_mate(d)
            pltpu.make_async_remote_copy(
                src_ref=one_sec.at[k, c, ss], dst_ref=one_sec.at[k, c, ss],
                send_sem=one_send.at[k, c], recv_sem=one_recv.at[k, c],
                device_id=at_slab(mate), device_id_type=MESH,
            ).start()

    def wait_bytes(sem, block):
        pltpu.make_async_copy(block, block, sem).wait()

    def combine(k, c):
        wait_bytes(one_recv.at[k, c], one_sec.at[k, c, pl.ds(0, slab - 1)])
        total = jnp.zeros((8, LANES), F32)
        weighted = total
        own = total
        for s in range(slab):
            tile = one_sec[k, c, s]
            swapped = turn(tile)
            total += tile
            weighted += zlow[s, 0] * tile + zlow[s, 1] * swapped
            own += zmin[s, 0] * tile + zmin[s, 1] * swapped
        if k:
            shift = cmul((zpre[zz, 0], zpre[zz, 1]), total)
            weighted += shift
            own += shift
        two_src[k, c, 0] = total
        two_src[k, c, 1] = weighted
        two_own[k, c, 0] = total
        two_own[k, c, 1] = own
        for d in far:
            other = lax.rem(zz + d, slabs)
            if k:
                later = (other > zz).astype(jnp.int32)
                source = two_src.at[k, c, pl.ds(later, 1)]
                target = two_sec.at[k, c, zz, pl.ds(0, 1)]
            else:
                source = two_src.at[k, c]
                target = two_sec.at[k, c, zz]
            pltpu.make_async_remote_copy(
                src_ref=source, dst_ref=target,
                send_sem=two_send.at[k, c], recv_sem=two_recv.at[k, c],
                device_id=at_other(other), device_id_type=MESH,
            ).start()

    def tiles(k, c, count):
        if k:
            return two_sec.at[k, c, pl.ds(0, count), pl.ds(0, 1)]
        return two_sec.at[k, c, pl.ds(0, count)]

    def heads(k, c):
        wait_bytes(two_recv.at[k, c], tiles(k, c, slabs - 1))
        near = two_own[k, c, 1]
        beyond = jnp.zeros((8, LANES), F32)
        if not k:
            near += cmul((zpre[zz, 0], zpre[zz, 1]), two_own[k, c, 0])
        for z in range(slabs):
            tile = two_sec[k, c, z, 0]
            beyond += jnp.where(z > zz, tile, 0.0)
            if k:
                near += jnp.where(z < zz, tile, 0.0)
            else:
                given = cmul((zpre[z, 0], zpre[z, 1]), tile) + two_sec[k, c, z, 1]
                near += jnp.where(z < zz, given, 0.0)
        here = (zpre[zz, 0] + zlow[ss, 0], zpre[zz, 1] + zlow[ss, 1])
        return jnp.where(upper, 1.0, 0.0) - near - cmul(here, beyond)

    def products(k, c):
        if k < SWEEPS - 1:
            drop[c] = dot(wide[...], cur[c]) + dot(wlow[...], cur[c, 0:2 * LANES, :])
        else:
            dropl[c] = dot(cur[c], wlast[0:4 * LANES, :], ((0,), (0,))) + dot(
                cur[c, 0:2 * LANES, :], wlast[4 * LANES:6 * LANES, :], ((0,), (0,))
            )

    def sweep(k, c):
        currents(k, c, heads(k - 1, c) if k else None)
        send_one(k, c)
        products(k, c)

    def finish(c):
        head = heads(SWEEPS - 1, c).T
        at = lax.rem(node + offsets[c], nodes) * chunk
        for q in range(PASS):
            where = pl.ds(pl.multiple_of(at + q * LANES, LANES), LANES)
            lo = q * LANES
            out_r[where, :] = head[:, q:q + 1] - dropl[c, lo:lo + LANES, 0:LANES]
            out_i[where, :] = head[:, q + 4:q + 5] - dropl[c, lo:lo + LANES, LANES:2 * LANES]

    mine = pl.ds(pl.multiple_of(core * half, half), half)

    def give(c):
        return pltpu.make_async_remote_copy(
            src_ref=fac.at[0, mine], dst_ref=fac.at[c, mine],
            send_sem=fac_send.at[c], recv_sem=fac_recv.at[c],
            device_id=at_node(nodes - offsets[c]), device_id_type=MESH,
        )

    def pass_on(c):
        return pltpu.make_async_remote_copy(
            src_ref=fac.at[c, mine], dst_ref=fac.at[c, mine],
            send_sem=pair_send.at[c], recv_sem=pair_recv.at[c],
            device_id={"feeder": partner, "node": node}, device_id_type=MESH,
        )

    level(0)
    currents(0, 0, None)
    pl.semaphore_wait(barrier, greeted)
    for d in wide_turns:
        pltpu.make_async_remote_copy(
            src_ref=zsec.at[ss], dst_ref=zsec.at[ss], send_sem=zs_send, recv_sem=zs_recv,
            device_id=at_slab(slab_mate(d)), device_id_type=MESH,
        ).start()
    send_one(0, 0)
    for c in range(1, nodes):
        give(c).start()

    width = LANES
    down = lax.broadcasted_iota(jnp.int32, (width, width), 0)
    across = lax.broadcasted_iota(jnp.int32, (width, width), 1)
    adjacent = jnp.where(jnp.broadcast_to(par_v[...], (width, width)) == down, 1.0, 0.0).T
    paths = jnp.where(down == across, 1.0, 0.0) + adjacent
    power = adjacent.astype(BF16)
    for turn_ in range((width - 1).bit_length() - 1):
        power = dot(power, power).astype(BF16)
        paths = paths + dot(paths.astype(BF16), power)
    paths_low = paths.astype(BF16)
    for part in range(2):
        z_row = jnp.broadcast_to(latz_v[part:part + 1, :], (width, width))
        z_high, z_mid = halves(z_row)
        z_low = (z_row - z_high.astype(F32) - z_mid.astype(F32)).astype(BF16)
        table = jnp.zeros((width, width), F32)
        for piece in (z_low, z_mid, z_high):
            table += dot((paths * piece.astype(F32)).astype(BF16), paths_low, ((1,), (1,)))
        prep[part] = table
    for part, sign, r0, c0 in ((0, 1.0, 0, 0), (1, -1.0, 0, 1), (1, 1.0, 1, 0), (0, 1.0, 1, 1)):
        high, low = halves(prep[part] * sign)
        rs, cs = slice(r0 * width, (r0 + 1) * width), slice(c0 * width, (c0 + 1) * width)
        wide[rs, cs] = high
        wide[rs, (c0 + 2) * width:(c0 + 3) * width] = high
        wlow[rs, cs] = low
        ts, us = slice(c0 * width, (c0 + 1) * width), slice(r0 * width, (r0 + 1) * width)
        wlast[ts, us] = high
        wlast[(c0 + 2) * width:(c0 + 3) * width, us] = high
        wlast[(c0 + 4) * width:(c0 + 5) * width, us] = low

    wait_bytes(zs_recv, zsec.at[pl.ds(0, slab - 1)])
    run_r = jnp.zeros((8, LANES), F32)
    run_i = run_r
    cut_r = run_r
    cut_i = run_r
    for s in range(slab):
        run_r += zsec[s, 0]
        run_i += zsec[s, 1]
        cut_r += jnp.where(s <= ss, zsec[s, 0], 0.0)
        cut_i += jnp.where(s <= ss, zsec[s, 1], 0.0)
        zlow[s, 0] = run_r
        zlow[s, 1] = run_i
        zmin[s, 0] = cut_r
        zmin[s, 1] = cut_i
    ztot[zz, 0] = run_r
    ztot[zz, 1] = run_i
    for d in far:
        pltpu.make_async_remote_copy(
            src_ref=ztot.at[zz], dst_ref=ztot.at[zz], send_sem=zt_send, recv_sem=zt_recv,
            device_id=at_other(lax.rem(zz + d, slabs)), device_id_type=MESH,
        ).start()
    combine(0, 0)
    products(0, 0)

    def bring(c):
        give(c).wait_recv()
        pass_on(c).start()

    def begin(c):
        pass_on(c).wait_recv()
        level(c)
        sweep(0, c)

    bring(1)
    if nodes > 2:
        bring(2)
    begin(1)
    if nodes > 2:
        begin(2)
    combine(0, 1)
    if nodes > 2:
        combine(0, 2)
    for c in range(3, nodes):
        bring(c)
        begin(c)

    wait_bytes(zt_recv, ztot.at[pl.ds(0, slabs - 1)])
    run_r = jnp.zeros((8, LANES), F32)
    run_i = run_r
    for z in range(slabs):
        zpre[z, 0] = run_r
        zpre[z, 1] = run_i
        run_r += ztot[z, 0]
        run_i += ztot[z, 1]

    for k in range(1, SWEEPS + 1):
        last = k == SWEEPS
        step = finish if last else functools.partial(sweep, k)
        step(0)
        for c in range(3, nodes):
            combine(k - 1, c)
        if not last:
            combine(k, 0)
        step(1)
        if nodes > 2:
            step(2)
        if not last:
            combine(k, 1)
            if nodes > 2:
                combine(k, 2)
        for c in range(3, nodes):
            step(c)

    wait_bytes(zs_send, zsec.at[pl.ds(0, slab - 1)])
    wait_bytes(zt_send, ztot.at[pl.ds(0, slabs - 1)])
    for c in range(1, nodes):
        give(c).wait_send()
        pass_on(c).wait_send()
    for k in range(SWEEPS):
        for c in range(nodes):
            wait_bytes(one_send.at[k, c], one_sec.at[k, c, pl.ds(0, slab - 1)])
            wait_bytes(two_send.at[k, c], tiles(k, c, slabs - 1))


def local(slabs, slab, nodes, factors, loadings, parents, load_base, lateral_z, trunk_z):
    chunk, depth = factors.shape
    scen = chunk * nodes
    width = loadings.shape[0]
    any_space = pl.BlockSpec(memory_space=pl.ANY)
    dma = pltpu.SemaphoreType.DMA
    out = jax.ShapeDtypeStruct((scen, width), F32)
    tile = (8, LANES)
    return pl.pallas_call(
        functools.partial(body, slabs, slab, nodes),
        out_shape=(out, out),
        in_specs=[any_space] * 5 + [pl.BlockSpec(memory_space=pltpu.SMEM)],
        out_specs=(pl.BlockSpec(memory_space=pltpu.VMEM),) * 2,
        scratch_shapes=[
            pltpu.VMEM((nodes, chunk, depth), BF16),
            pltpu.VMEM((nodes, width, chunk), F32),
            pltpu.VMEM((nodes, 4 * width, chunk), BF16),
            pltpu.VMEM((nodes, 2 * width, chunk), F32),
            pltpu.VMEM((nodes, chunk, 2 * width), F32),
            pltpu.VMEM((2 * width, 4 * width), BF16),
            pltpu.VMEM((2 * width, 2 * width), BF16),
            pltpu.VMEM((6 * width, 2 * width), BF16),
            pltpu.VMEM((width, LANES), F32),
            pltpu.VMEM((width, LANES), F32),
            pltpu.VMEM((SWEEPS, nodes, slab) + tile, F32),
            pltpu.VMEM((SWEEPS, nodes, slabs, 2) + tile, F32),
            pltpu.VMEM((SWEEPS, nodes, 2) + tile, F32),
            pltpu.VMEM((SWEEPS, nodes, 2) + tile, F32),
            pltpu.VMEM((slab, 2) + tile, F32),
            pltpu.VMEM((slab, 2) + tile, F32),
            pltpu.VMEM((slab, 2) + tile, F32),
            pltpu.VMEM((slabs, 2) + tile, F32),
            pltpu.VMEM((slabs, 2) + tile, F32),
            pltpu.VMEM((2, width, width), F32),
            pltpu.VMEM((width, depth), BF16),
            pltpu.VMEM((1, width), jnp.int32),
            pltpu.VMEM((2, width), F32),
            pltpu.VMEM((2, width), F32),
            dma((5,)),
            dma((nodes,)),
            dma((nodes,)),
            dma((nodes,)),
            dma((nodes,)),
            dma(()),
            dma(()),
            dma(()),
            dma(()),
            dma((SWEEPS, nodes)),
            dma((SWEEPS, nodes)),
            dma((SWEEPS, nodes)),
            dma((SWEEPS, nodes)),
        ],
        compiler_params=pltpu.CompilerParams(
            collective_id=0, has_side_effects=True, vmem_limit_bytes=48 * 1024 * 1024
        ),
    )(factors, loadings, parents.reshape(1, width), load_base, lateral_z, trunk_z.reshape(2))


def solution(mesh):
    feeder = mesh.shape["feeder"]
    slab = 8 if feeder >= 64 else 2
    return jax.shard_map(
        functools.partial(local, feeder // slab, slab, mesh.shape["node"]),
        mesh=mesh,
        in_specs=(
            P("node", None),
            P(("feeder", "node"), None),
            P(("feeder", "node")),
            P(None, ("feeder", "node")),
            P(None, ("feeder", "node")),
            P(None, "feeder", "node"),
        ),
        out_specs=(P(None, ("feeder", "node")), P(None, ("feeder", "node"))),
        check_vma=False,
    )
```

```python
import functools

import jax
import jax.numpy as jnp
from jax import lax
from jax.experimental import pallas as pl
from jax.experimental.pallas import tpu as pltpu
from jax.sharding import PartitionSpec as P

MESH = pl.DeviceIdType.MESH
F32 = jnp.float32
BF16 = jnp.bfloat16
SWEEPS = 3
LANES = 128
ORDER = (
    "L0 C00 X P",
    "S B00",
    "G1 G2",
    "L1 A01",
    "L2 A02",
    "G3 M00 M01",
    "L3 A03",
    "M02 M03",
    "Z A10 B01",
    "B02 B03 M10 B10",
    "A11 A12 A13",
    "M11 M12 M13",
    "A20 B11 B12 B13",
    "M20 B20",
    "A21 A22 A23",
    "M21 M22 M23",
    "F0 B21 B22 B23",
    "F1 F2 F3",
)
PIECES = 4
PASS = 4


def dot(a, b, dims=((1,), (0,))):
    return lax.dot_general(a, b, (dims, ((), ())), preferred_element_type=F32)


def halves(value):
    high = value.astype(BF16)
    return high, (value - high.astype(F32)).astype(BF16)


def turn(tile):
    return pltpu.roll(tile, 4, 0)


def cmul(ratio, tile):
    return ratio[0] * tile + ratio[1] * turn(tile)


def body(
    slabs, slab, nodes, fac_ref, load_ref, par_ref, base_ref, latz_ref, trz_ref, out_r, out_i,
    fac, swing, cur, drop, dropl, wide, wlow, wlast, pcol, qcol, one_sec, two_sec, two_src, two_own,
    zsec, zlow, zmin, ztot, zpre, prep,
    load_v, par_v, base_v, latz_v, trz_s,
    local_sem, fac_send, fac_recv, pair_send, pair_recv, zs_send, zs_recv, zt_send, zt_recv,
    one_send, one_recv, two_send, two_recv,
):
    feeder = lax.axis_index("feeder")
    node = lax.axis_index("node")
    zz = feeder // slab
    ss = lax.rem(feeder, slab)
    core = lax.rem(feeder, 2)
    partner = feeder + 1 - 2 * core
    chunk = fac.shape[1]
    half = chunk // 2
    offsets = [0, 1, nodes - 1] + [o for o in range(2, nodes - 1)]

    def slab_mate(turn_):
        return lax.rem(ss + turn_, slab)

    def at_slab(mate):
        return {"feeder": zz * slab + mate, "node": node}

    def at_other(other):
        return {"feeder": other * slab + ss, "node": node}

    def at_node(offset):
        return {"feeder": feeder, "node": lax.rem(node + offset, nodes)}

    far = sorted(range(1, slabs), key=lambda d: -min(d, slabs - d))
    wide_turns = sorted(range(1, slab), key=lambda d: -min(d, slab - d))

    barrier = pltpu.get_barrier_semaphore()
    greeted = 0
    for d in far:
        pl.semaphore_signal(barrier, inc=1, device_id=at_other(lax.rem(zz + d, slabs)), device_id_type=MESH)
        greeted += 1
    for d in wide_turns:
        pl.semaphore_signal(barrier, inc=1, device_id=at_slab(slab_mate(d)), device_id_type=MESH)
        greeted += 1
    for o in offsets[1:]:
        pl.semaphore_signal(barrier, inc=1, device_id=at_node(o), device_id_type=MESH)
        greeted += 1

    copies = [
        pltpu.make_async_copy(fac_ref, fac.at[0], local_sem.at[0]),
        pltpu.make_async_copy(load_ref, load_v, local_sem.at[1]),
        pltpu.make_async_copy(base_ref, base_v, local_sem.at[2]),
        pltpu.make_async_copy(par_ref, par_v, local_sem.at[3]),
        pltpu.make_async_copy(latz_ref, latz_v, local_sem.at[4]),
        pltpu.make_async_copy(trz_ref, trz_s, local_sem.at[5]),
    ]
    for copy in copies:
        copy.start()
    for copy in copies:
        copy.wait()

    pcol[...] = jnp.broadcast_to(base_v[0:1, :], (LANES, LANES)).T
    qcol[...] = jnp.broadcast_to(base_v[1:2, :], (LANES, LANES)).T
    row8 = lax.broadcasted_iota(jnp.int32, (8, LANES), 0)
    upper = row8 < 4
    z_real = trz_s[0]
    z_imag = trz_s[1]
    zsec[ss, 0] = jnp.zeros((8, LANES), F32) + z_real
    zsec[ss, 1] = jnp.where(upper, -z_imag, z_imag)

    def level(c):
        for q in range(PASS):
            lo = q * LANES
            lev = dot(load_v[...], fac[c, lo:lo + LANES, :], ((1,), (1,)))
            swing[c, :, lo:lo + LANES] = 1.0 + 0.5 * jnp.tanh(lev.astype(BF16).astype(F32))

    rows = 16

    def currents(k, c, head):
        for q in range(PASS):
            lo = q * LANES
            if k:
                head_r = jnp.broadcast_to(head[q:q + 1, :], (rows, LANES))
                head_i = jnp.broadcast_to(head[q + 4:q + 5, :], (rows, LANES))

            def step(i, sums):
                at = pl.multiple_of(i * rows, rows)
                sw = swing[c, pl.ds(at, rows), lo:lo + LANES]
                p = pcol[pl.ds(at, rows), :]
                r = qcol[pl.ds(at, rows), :]
                if k:
                    vr = head_r - drop[c, pl.ds(at, rows), lo:lo + LANES]
                    vi = head_i - drop[c, pl.ds(LANES + at, rows), lo:lo + LANES]
                    t = sw / (vr * vr + vi * vi)
                    cr = t * (p * vr + r * vi)
                    ci = t * (p * vi - r * vr)
                else:
                    cr = sw * p
                    ci = -(sw * r)
                for part, value in ((0, cr), (1, ci)):
                    high, low = halves(value)
                    cur[c, pl.ds(part * LANES + at, rows), lo:lo + LANES] = high
                    cur[c, pl.ds((part + 2) * LANES + at, rows), lo:lo + LANES] = low
                return (
                    sums[0] + cr[0:8] + cr[8:16],
                    sums[1] + ci[0:8] + ci[8:16],
                )

            zero = jnp.zeros((8, LANES), F32)
            sum_r, sum_i = lax.fori_loop(0, LANES // rows, step, (zero, zero), unroll=4)
            one_sec[k, c, ss, q:q + 1, :] = jnp.sum(sum_r, axis=0, keepdims=True)
            one_sec[k, c, ss, q + 4:q + 5, :] = jnp.sum(sum_i, axis=0, keepdims=True)

    def send_one(k, c):
        for d in wide_turns:
            mate = slab_mate(d)
            pltpu.make_async_remote_copy(
                src_ref=one_sec.at[k, c, ss], dst_ref=one_sec.at[k, c, ss],
                send_sem=one_send.at[k, c], recv_sem=one_recv.at[k, c],
                device_id=at_slab(mate), device_id_type=MESH,
            ).start()

    def wait_bytes(sem, block):
        pltpu.make_async_copy(block, block, sem).wait()

    def combine(k, c):
        wait_bytes(one_recv.at[k, c], one_sec.at[k, c, pl.ds(0, slab - 1)])
        total = jnp.zeros((8, LANES), F32)
        weighted = total
        own = total
        for s in range(slab):
            tile = one_sec[k, c, s]
            swapped = turn(tile)
            total += tile
            weighted += zlow[s, 0] * tile + zlow[s, 1] * swapped
            own += zmin[s, 0] * tile + zmin[s, 1] * swapped
        if k:
            shift = cmul((zpre[zz, 0], zpre[zz, 1]), total)
            weighted += shift
            own += shift
        two_src[k, c, 0] = total
        two_src[k, c, 1] = weighted
        two_own[k, c, 0] = total
        two_own[k, c, 1] = own
        for d in far:
            other = lax.rem(zz + d, slabs)
            if k:
                later = (other > zz).astype(jnp.int32)
                source = two_src.at[k, c, pl.ds(later, 1)]
                target = two_sec.at[k, c, zz, pl.ds(0, 1)]
            else:
                source = two_src.at[k, c]
                target = two_sec.at[k, c, zz]
            pltpu.make_async_remote_copy(
                src_ref=source, dst_ref=target,
                send_sem=two_send.at[k, c], recv_sem=two_recv.at[k, c],
                device_id=at_other(other), device_id_type=MESH,
            ).start()

    def tiles(k, c, count):
        if k:
            return two_sec.at[k, c, pl.ds(0, count), pl.ds(0, 1)]
        return two_sec.at[k, c, pl.ds(0, count)]

    def heads(k, c):
        wait_bytes(two_recv.at[k, c], tiles(k, c, slabs - 1))
        near = two_own[k, c, 1]
        beyond = jnp.zeros((8, LANES), F32)
        if not k:
            near += cmul((zpre[zz, 0], zpre[zz, 1]), two_own[k, c, 0])
        for z in range(slabs):
            tile = two_sec[k, c, z, 0]
            beyond += jnp.where(z > zz, tile, 0.0)
            if k:
                near += jnp.where(z < zz, tile, 0.0)
            else:
                given = cmul((zpre[z, 0], zpre[z, 1]), tile) + two_sec[k, c, z, 1]
                near += jnp.where(z < zz, given, 0.0)
        here = (zpre[zz, 0] + zlow[ss, 0], zpre[zz, 1] + zlow[ss, 1])
        return jnp.where(upper, 1.0, 0.0) - near - cmul(here, beyond)

    def products(k, c):
        if k < SWEEPS - 1:
            drop[c] = dot(wide[...], cur[c]) + dot(wlow[...], cur[c, 0:2 * LANES, :])
        else:
            dropl[c] = dot(cur[c], wlast[0:4 * LANES, :], ((0,), (0,))) + dot(
                cur[c, 0:2 * LANES, :], wlast[4 * LANES:6 * LANES, :], ((0,), (0,))
            )

    def finish(c):
        head = heads(SWEEPS - 1, c).T
        at = lax.rem(node + offsets[c], nodes) * chunk
        for q in range(PASS):
            where = pl.ds(pl.multiple_of(at + q * LANES, LANES), LANES)
            lo = q * LANES
            out_r[where, :] = head[:, q:q + 1] - dropl[c, lo:lo + LANES, 0:LANES]
            out_i[where, :] = head[:, q + 4:q + 5] - dropl[c, lo:lo + LANES, LANES:2 * LANES]

    mine = pl.ds(pl.multiple_of(core * half, half), half)

    def give(c):
        return pltpu.make_async_remote_copy(
            src_ref=fac.at[0, mine], dst_ref=fac.at[c, mine],
            send_sem=fac_send.at[c], recv_sem=fac_recv.at[c],
            device_id=at_node(nodes - offsets[c]), device_id_type=MESH,
        )

    def pass_on(c):
        return pltpu.make_async_remote_copy(
            src_ref=fac.at[c, mine], dst_ref=fac.at[c, mine],
            send_sem=pair_send.at[c], recv_sem=pair_recv.at[c],
            device_id={"feeder": partner, "node": node}, device_id_type=MESH,
        )

    def open_up():
        pl.semaphore_wait(barrier, greeted)
        for d in wide_turns:
            pltpu.make_async_remote_copy(
                src_ref=zsec.at[ss], dst_ref=zsec.at[ss], send_sem=zs_send, recv_sem=zs_recv,
                device_id=at_slab(slab_mate(d)), device_id_type=MESH,
            ).start()
        send_one(0, 0)
        for c in range(1, min(nodes, 3)):
            give(c).start()

    def tables():
        width = LANES
        down = lax.broadcasted_iota(jnp.int32, (width, width), 0)
        across = lax.broadcasted_iota(jnp.int32, (width, width), 1)
        adjacent = jnp.where(jnp.broadcast_to(par_v[...], (width, width)) == down, 1.0, 0.0).T
        paths = jnp.where(down == across, 1.0, 0.0) + adjacent
        power = adjacent.astype(BF16)
        for turn_ in range((width - 1).bit_length() - 1):
            power = dot(power, power).astype(BF16)
            paths = paths + dot(paths.astype(BF16), power)
        paths_low = paths.astype(BF16)
        for part in range(2):
            z_row = jnp.broadcast_to(latz_v[part:part + 1, :], (width, width))
            z_high, z_mid = halves(z_row)
            z_low = (z_row - z_high.astype(F32) - z_mid.astype(F32)).astype(BF16)
            table = jnp.zeros((width, width), F32)
            for piece in (z_low, z_mid, z_high):
                table += dot((paths * piece.astype(F32)).astype(BF16), paths_low, ((1,), (1,)))
            prep[part] = table
        for part, sign, r0, c0 in ((0, 1.0, 0, 0), (1, -1.0, 0, 1), (1, 1.0, 1, 0), (0, 1.0, 1, 1)):
            high, low = halves(prep[part] * sign)
            rs, cs = slice(r0 * width, (r0 + 1) * width), slice(c0 * width, (c0 + 1) * width)
            wide[rs, cs] = high
            wide[rs, (c0 + 2) * width:(c0 + 3) * width] = high
            wlow[rs, cs] = low
            ts, us = slice(c0 * width, (c0 + 1) * width), slice(r0 * width, (r0 + 1) * width)
            wlast[ts, us] = high
            wlast[(c0 + 2) * width:(c0 + 3) * width, us] = high
            wlast[(c0 + 4) * width:(c0 + 5) * width, us] = low

    def slab_z():
        wait_bytes(zs_recv, zsec.at[pl.ds(0, slab - 1)])
        run_r = jnp.zeros((8, LANES), F32)
        run_i = run_r
        cut_r = run_r
        cut_i = run_r
        for s in range(slab):
            run_r += zsec[s, 0]
            run_i += zsec[s, 1]
            cut_r += jnp.where(s <= ss, zsec[s, 0], 0.0)
            cut_i += jnp.where(s <= ss, zsec[s, 1], 0.0)
            zlow[s, 0] = run_r
            zlow[s, 1] = run_i
            zmin[s, 0] = cut_r
            zmin[s, 1] = cut_i
        ztot[zz, 0] = run_r
        ztot[zz, 1] = run_i
        for d in far:
            pltpu.make_async_remote_copy(
                src_ref=ztot.at[zz], dst_ref=ztot.at[zz], send_sem=zt_send, recv_sem=zt_recv,
                device_id=at_other(lax.rem(zz + d, slabs)), device_id_type=MESH,
            ).start()
    def trunk_z():
        wait_bytes(zt_recv, ztot.at[pl.ds(0, slabs - 1)])
        run_r = jnp.zeros((8, LANES), F32)
        run_i = run_r
        for z in range(slabs):
            zpre[z, 0] = run_r
            zpre[z, 1] = run_i
            run_r += ztot[z, 0]
            run_i += ztot[z, 1]

    def do(name):
        if name == "P":
            tables()
            for c in range(3, nodes):
                give(c).start()
        elif name == "S":
            slab_z()
        elif name == "Z":
            trunk_z()
        elif name == "X":
            open_up()
        elif name[0] == "G":
            give(int(name[1])).wait_recv()
            pass_on(int(name[1])).start()
        elif name[0] == "L":
            c = int(name[1])
            if c:
                pass_on(c).wait_recv()
            level(c)
        elif name[0] == "F":
            finish(int(name[1]))
        else:
            k, c = int(name[1]), int(name[2])
            if name[0] in "AC":
                currents(k, c, heads(k - 1, c) if k else None)
            if name[0] == "A":
                send_one(k, c)
            if name[0] == "M":
                products(k, c)
            if name[0] == "B":
                combine(k, c)

    for line in ORDER:
        for name in line.split():
            if int(name[-1] if name[-1].isdigit() else 0) < nodes:
                do(name)

    wait_bytes(zs_send, zsec.at[pl.ds(0, slab - 1)])
    wait_bytes(zt_send, ztot.at[pl.ds(0, slabs - 1)])
    for c in range(1, nodes):
        give(c).wait_send()
        pass_on(c).wait_send()
    for k in range(SWEEPS):
        for c in range(nodes):
            wait_bytes(one_send.at[k, c], one_sec.at[k, c, pl.ds(0, slab - 1)])
            wait_bytes(two_send.at[k, c], tiles(k, c, slabs - 1))


def store(in_r, in_i, out_r, out_i, sem):
    rows = in_r.shape[0] // PIECES
    copies = []
    for p in range(PIECES):
        where = pl.ds(p * rows, rows)
        copies.append(pltpu.make_async_copy(in_r.at[where], out_r.at[where], sem.at[0, p]))
        copies.append(pltpu.make_async_copy(in_i.at[where], out_i.at[where], sem.at[1, p]))
    for copy in copies:
        copy.start()
    for copy in copies:
        copy.wait()


def local(slabs, slab, nodes, factors, loadings, parents, load_base, lateral_z, trunk_z):
    chunk, depth = factors.shape
    scen = chunk * nodes
    width = loadings.shape[0]
    any_space = pl.BlockSpec(memory_space=pltpu.HBM)
    dma = pltpu.SemaphoreType.DMA
    hbm = functools.partial(pltpu.with_memory_space_constraint, memory_space=pltpu.HBM)
    out = jax.ShapeDtypeStruct((scen, width), F32)
    tile = (8, LANES)
    volts = pl.pallas_call(
        functools.partial(body, slabs, slab, nodes),
        out_shape=(out, out),
        in_specs=[any_space] * 6,
        out_specs=(pl.BlockSpec(memory_space=pltpu.VMEM),) * 2,
        scratch_shapes=[
            pltpu.VMEM((nodes, chunk, depth), BF16),
            pltpu.VMEM((nodes, width, chunk), F32),
            pltpu.VMEM((nodes, 4 * width, chunk), BF16),
            pltpu.VMEM((nodes, 2 * width, chunk), F32),
            pltpu.VMEM((nodes, chunk, 2 * width), F32),
            pltpu.VMEM((2 * width, 4 * width), BF16),
            pltpu.VMEM((2 * width, 2 * width), BF16),
            pltpu.VMEM((6 * width, 2 * width), BF16),
            pltpu.VMEM((width, LANES), F32),
            pltpu.VMEM((width, LANES), F32),
            pltpu.VMEM((SWEEPS, nodes, slab) + tile, F32),
            pltpu.VMEM((SWEEPS, nodes, slabs, 2) + tile, F32),
            pltpu.VMEM((SWEEPS, nodes, 2) + tile, F32),
            pltpu.VMEM((SWEEPS, nodes, 2) + tile, F32),
            pltpu.VMEM((slab, 2) + tile, F32),
            pltpu.VMEM((slab, 2) + tile, F32),
            pltpu.VMEM((slab, 2) + tile, F32),
            pltpu.VMEM((slabs, 2) + tile, F32),
            pltpu.VMEM((slabs, 2) + tile, F32),
            pltpu.VMEM((2, width, width), F32),
            pltpu.VMEM((width, depth), BF16),
            pltpu.VMEM((1, width), jnp.int32),
            pltpu.VMEM((2, width), F32),
            pltpu.VMEM((2, width), F32),
            pltpu.SMEM((2,), F32),
            dma((6,)),
            dma((nodes,)),
            dma((nodes,)),
            dma((nodes,)),
            dma((nodes,)),
            dma(()),
            dma(()),
            dma(()),
            dma(()),
            dma((SWEEPS, nodes)),
            dma((SWEEPS, nodes)),
            dma((SWEEPS, nodes)),
            dma((SWEEPS, nodes)),
        ],
        compiler_params=pltpu.CompilerParams(
            collective_id=0, has_side_effects=True, vmem_limit_bytes=48 * 1024 * 1024
        ),
    )(*[hbm(a) for a in (factors, loadings, parents.reshape(1, width), load_base, lateral_z, trunk_z.reshape(2))])
    return pl.pallas_call(
        store,
        out_shape=(out, out),
        in_specs=[pl.BlockSpec(memory_space=pltpu.VMEM)] * 2,
        out_specs=(any_space,) * 2,
        scratch_shapes=[dma((2, PIECES))],
        compiler_params=pltpu.CompilerParams(vmem_limit_bytes=1024 * 1024),
    )(*volts)


def solution(mesh):
    feeder = mesh.shape["feeder"]
    slab = 8 if feeder >= 64 else 2
    return jax.shard_map(
        functools.partial(local, feeder // slab, slab, mesh.shape["node"]),
        mesh=mesh,
        in_specs=(
            P("node", None),
            P(("feeder", "node"), None),
            P(("feeder", "node")),
            P(None, ("feeder", "node")),
            P(None, ("feeder", "node")),
            P(None, "feeder", "node"),
        ),
        out_specs=(P(None, ("feeder", "node")), P(None, ("feeder", "node"))),
        check_vma=False,
    )
```

```python
import functools

import jax
import jax.numpy as jnp
from jax import lax
from jax.experimental import pallas as pl
from jax.experimental.pallas import tpu as pltpu
from jax.sharding import PartitionSpec as P

MESH = pl.DeviceIdType.MESH
F32 = jnp.float32
BF16 = jnp.bfloat16
SWEEPS = 3
LANES = 128
ORDER = (
    "L0 C00 X P",
    "S B00",
    "G1 G2",
    "L1 A01",
    "L2 A02",
    "G3 M00 M01",
    "L3 A03",
    "M02 M03",
    "Z A10 B01",
    "B02 B03 M10 B10",
    "A11 A12 A13",
    "M11 M12 M13",
    "A20 B11 B12 B13",
    "M20 B20",
    "A21 A22 A23",
    "M21 M22 M23",
    "F0 B21 B22 B23",
    "F1 F2 F3",
)
PIECES = 4
PASS = 4


def dot(a, b, dims=((1,), (0,))):
    return lax.dot_general(a, b, (dims, ((), ())), preferred_element_type=F32)


def halves(value):
    high = value.astype(BF16)
    return high, (value - high.astype(F32)).astype(BF16)


def turn(tile):
    return pltpu.roll(tile, 4, 0)


def cmul(ratio, tile):
    return ratio[0] * tile + ratio[1] * turn(tile)


def body(
    slabs, slab, nodes, fac_ref, load_ref, par_ref, base_ref, latz_ref, trz_ref, out_r, out_i,
    fac, swing, cur, drop, dropl, wide, wlow, wlast, pcol, qcol, one_sec, two_sec, two_src, two_own,
    zsec, zlow, zmin, ztot, zpre, prep,
    load_v, par_v, base_v, latz_v, trz_s,
    local_sem, fac_send, fac_recv, pair_send, pair_recv, zs_send, zs_recv, zt_send, zt_recv,
    one_send, one_recv, two_send, two_recv,
):
    feeder = lax.axis_index("feeder")
    node = lax.axis_index("node")
    zz = feeder // slab
    ss = lax.rem(feeder, slab)
    core = lax.rem(feeder, 2)
    partner = feeder + 1 - 2 * core
    chunk = fac.shape[1]
    half = chunk // 2
    offsets = [0, 1, nodes - 1] + [o for o in range(2, nodes - 1)]

    def slab_mate(turn_):
        return lax.rem(ss + turn_, slab)

    def at_slab(mate):
        return {"feeder": zz * slab + mate, "node": node}

    def at_other(other):
        return {"feeder": other * slab + ss, "node": node}

    def at_node(offset):
        return {"feeder": feeder, "node": lax.rem(node + offset, nodes)}

    far = sorted(range(1, slabs), key=lambda d: -min(d, slabs - d))
    wide_turns = sorted(range(1, slab), key=lambda d: -min(d, slab - d))

    barrier = pltpu.get_barrier_semaphore()
    greeted = 0
    for d in far:
        pl.semaphore_signal(barrier, inc=1, device_id=at_other(lax.rem(zz + d, slabs)), device_id_type=MESH)
        greeted += 1
    for d in wide_turns:
        pl.semaphore_signal(barrier, inc=1, device_id=at_slab(slab_mate(d)), device_id_type=MESH)
        greeted += 1
    for o in offsets[1:]:
        pl.semaphore_signal(barrier, inc=1, device_id=at_node(o), device_id_type=MESH)
        greeted += 1

    copies = [
        pltpu.make_async_copy(fac_ref, fac.at[0], local_sem.at[0]),
        pltpu.make_async_copy(load_ref, load_v, local_sem.at[1]),
        pltpu.make_async_copy(base_ref, base_v, local_sem.at[2]),
        pltpu.make_async_copy(par_ref, par_v, local_sem.at[3]),
        pltpu.make_async_copy(latz_ref, latz_v, local_sem.at[4]),
        pltpu.make_async_copy(trz_ref, trz_s, local_sem.at[5]),
    ]
    for copy in copies:
        copy.start()
    for copy in copies:
        copy.wait()

    pcol[...] = jnp.broadcast_to(base_v[0:1, :], (LANES, LANES)).T
    qcol[...] = jnp.broadcast_to(base_v[1:2, :], (LANES, LANES)).T
    row8 = lax.broadcasted_iota(jnp.int32, (8, LANES), 0)
    upper = row8 < 4
    z_real = trz_s[0]
    z_imag = trz_s[1]
    zsec[ss, 0] = jnp.zeros((8, LANES), F32) + z_real
    zsec[ss, 1] = jnp.where(upper, -z_imag, z_imag)

    def level(c):
        for q in range(PASS):
            lo = q * LANES
            lev = dot(load_v[...], fac[c, lo:lo + LANES, :], ((1,), (1,)))
            swing[c, :, lo:lo + LANES] = 1.0 + 0.5 * jnp.tanh(lev.astype(BF16).astype(F32))

    rows = 16

    def currents(k, c, head):
        for q in range(PASS):
            lo = q * LANES
            if k:
                head_r = jnp.broadcast_to(head[q:q + 1, :], (rows, LANES))
                head_i = jnp.broadcast_to(head[q + 4:q + 5, :], (rows, LANES))

            def step(i, sums):
                at = pl.multiple_of(i * rows, rows)
                sw = swing[c, pl.ds(at, rows), lo:lo + LANES]
                p = pcol[pl.ds(at, rows), :]
                r = qcol[pl.ds(at, rows), :]
                if k:
                    vr = head_r - drop[c, pl.ds(at, rows), lo:lo + LANES]
                    vi = head_i - drop[c, pl.ds(LANES + at, rows), lo:lo + LANES]
                    t = sw / (vr * vr + vi * vi)
                    cr = t * (p * vr + r * vi)
                    ci = t * (p * vi - r * vr)
                else:
                    cr = sw * p
                    ci = -(sw * r)
                for part, value in ((0, cr), (1, ci)):
                    high, low = halves(value)
                    cur[c, pl.ds(part * LANES + at, rows), lo:lo + LANES] = high
                    cur[c, pl.ds((part + 2) * LANES + at, rows), lo:lo + LANES] = low
                return (
                    sums[0] + cr[0:8] + cr[8:16],
                    sums[1] + ci[0:8] + ci[8:16],
                )

            zero = jnp.zeros((8, LANES), F32)
            sum_r, sum_i = lax.fori_loop(0, LANES // rows, step, (zero, zero), unroll=4)
            one_sec[k, c, ss, q:q + 1, :] = jnp.sum(sum_r, axis=0, keepdims=True)
            one_sec[k, c, ss, q + 4:q + 5, :] = jnp.sum(sum_i, axis=0, keepdims=True)

    def send_one(k, c):
        for d in wide_turns:
            mate = slab_mate(d)
            pltpu.make_async_remote_copy(
                src_ref=one_sec.at[k, c, ss], dst_ref=one_sec.at[k, c, ss],
                send_sem=one_send.at[k, c], recv_sem=one_recv.at[k, c],
                device_id=at_slab(mate), device_id_type=MESH,
            ).start()

    def wait_bytes(sem, block):
        pltpu.make_async_copy(block, block, sem).wait()

    def combine(k, c):
        wait_bytes(one_recv.at[k, c], one_sec.at[k, c, pl.ds(0, slab - 1)])
        total = jnp.zeros((8, LANES), F32)
        weighted = total
        own = total
        for s in range(slab):
            tile = one_sec[k, c, s]
            swapped = turn(tile)
            total += tile
            weighted += zlow[s, 0] * tile + zlow[s, 1] * swapped
            own += zmin[s, 0] * tile + zmin[s, 1] * swapped
        if k or c:
            shift = cmul((zpre[zz, 0], zpre[zz, 1]), total)
            weighted += shift
            own += shift
        two_src[k, c, 0] = total
        two_src[k, c, 1] = weighted
        two_own[k, c, 0] = total
        two_own[k, c, 1] = own
        for d in far:
            other = lax.rem(zz + d, slabs)
            if k or c:
                later = (other > zz).astype(jnp.int32)
                source = two_src.at[k, c, pl.ds(later, 1)]
                target = two_sec.at[k, c, zz, pl.ds(0, 1)]
            else:
                source = two_src.at[k, c]
                target = two_sec.at[k, c, zz]
            pltpu.make_async_remote_copy(
                src_ref=source, dst_ref=target,
                send_sem=two_send.at[k, c], recv_sem=two_recv.at[k, c],
                device_id=at_other(other), device_id_type=MESH,
            ).start()

    def tiles(k, c, count):
        if k or c:
            return two_sec.at[k, c, pl.ds(0, count), pl.ds(0, 1)]
        return two_sec.at[k, c, pl.ds(0, count)]

    def heads(k, c):
        wait_bytes(two_recv.at[k, c], tiles(k, c, slabs - 1))
        near = two_own[k, c, 1]
        beyond = jnp.zeros((8, LANES), F32)
        if not (k or c):
            near += cmul((zpre[zz, 0], zpre[zz, 1]), two_own[k, c, 0])
        for z in range(slabs):
            tile = two_sec[k, c, z, 0]
            beyond += jnp.where(z > zz, tile, 0.0)
            if k or c:
                near += jnp.where(z < zz, tile, 0.0)
            else:
                given = cmul((zpre[z, 0], zpre[z, 1]), tile) + two_sec[k, c, z, 1]
                near += jnp.where(z < zz, given, 0.0)
        here = (zpre[zz, 0] + zlow[ss, 0], zpre[zz, 1] + zlow[ss, 1])
        return jnp.where(upper, 1.0, 0.0) - near - cmul(here, beyond)

    def products(k, c):
        if k < SWEEPS - 1:
            drop[c] = dot(wide[...], cur[c]) + dot(wlow[...], cur[c, 0:2 * LANES, :])
        else:
            dropl[c] = dot(cur[c], wlast[0:4 * LANES, :], ((0,), (0,))) + dot(
                cur[c, 0:2 * LANES, :], wlast[4 * LANES:6 * LANES, :], ((0,), (0,))
            )

    def finish(c):
        head = heads(SWEEPS - 1, c).T
        at = lax.rem(node + offsets[c], nodes) * chunk
        for q in range(PASS):
            where = pl.ds(pl.multiple_of(at + q * LANES, LANES), LANES)
            lo = q * LANES
            out_r[where, :] = head[:, q:q + 1] - dropl[c, lo:lo + LANES, 0:LANES]
            out_i[where, :] = head[:, q + 4:q + 5] - dropl[c, lo:lo + LANES, LANES:2 * LANES]

    mine = pl.ds(pl.multiple_of(core * half, half), half)

    def give(c):
        return pltpu.make_async_remote_copy(
            src_ref=fac.at[0, mine], dst_ref=fac.at[c, mine],
            send_sem=fac_send.at[c], recv_sem=fac_recv.at[c],
            device_id=at_node(nodes - offsets[c]), device_id_type=MESH,
        )

    def pass_on(c):
        return pltpu.make_async_remote_copy(
            src_ref=fac.at[c, mine], dst_ref=fac.at[c, mine],
            send_sem=pair_send.at[c], recv_sem=pair_recv.at[c],
            device_id={"feeder": partner, "node": node}, device_id_type=MESH,
        )

    def open_up():
        pl.semaphore_wait(barrier, greeted)
        for d in wide_turns:
            pltpu.make_async_remote_copy(
                src_ref=zsec.at[ss], dst_ref=zsec.at[ss], send_sem=zs_send, recv_sem=zs_recv,
                device_id=at_slab(slab_mate(d)), device_id_type=MESH,
            ).start()
        send_one(0, 0)
        for c in range(1, min(nodes, 3)):
            give(c).start()

    def tables():
        width = LANES
        down = lax.broadcasted_iota(jnp.int32, (width, width), 0)
        across = lax.broadcasted_iota(jnp.int32, (width, width), 1)
        adjacent = jnp.where(jnp.broadcast_to(par_v[...], (width, width)) == down, 1.0, 0.0).T
        paths = jnp.where(down == across, 1.0, 0.0) + adjacent
        power = adjacent.astype(BF16)
        for turn_ in range((width - 1).bit_length() - 1):
            power = dot(power, power).astype(BF16)
            paths = paths + dot(paths.astype(BF16), power)
        paths_low = paths.astype(BF16)
        for part in range(2):
            z_row = jnp.broadcast_to(latz_v[part:part + 1, :], (width, width))
            z_high, z_mid = halves(z_row)
            z_low = (z_row - z_high.astype(F32) - z_mid.astype(F32)).astype(BF16)
            table = jnp.zeros((width, width), F32)
            for piece in (z_low, z_mid, z_high):
                table += dot((paths * piece.astype(F32)).astype(BF16), paths_low, ((1,), (1,)))
            prep[part] = table
        for part, sign, r0, c0 in ((0, 1.0, 0, 0), (1, -1.0, 0, 1), (1, 1.0, 1, 0), (0, 1.0, 1, 1)):
            high, low = halves(prep[part] * sign)
            rs, cs = slice(r0 * width, (r0 + 1) * width), slice(c0 * width, (c0 + 1) * width)
            wide[rs, cs] = high
            wide[rs, (c0 + 2) * width:(c0 + 3) * width] = high
            wlow[rs, cs] = low
            ts, us = slice(c0 * width, (c0 + 1) * width), slice(r0 * width, (r0 + 1) * width)
            wlast[ts, us] = high
            wlast[(c0 + 2) * width:(c0 + 3) * width, us] = high
            wlast[(c0 + 4) * width:(c0 + 5) * width, us] = low

    def slab_z():
        wait_bytes(zs_recv, zsec.at[pl.ds(0, slab - 1)])
        run_r = jnp.zeros((8, LANES), F32)
        run_i = run_r
        cut_r = run_r
        cut_i = run_r
        for s in range(slab):
            run_r += zsec[s, 0]
            run_i += zsec[s, 1]
            cut_r += jnp.where(s <= ss, zsec[s, 0], 0.0)
            cut_i += jnp.where(s <= ss, zsec[s, 1], 0.0)
            zlow[s, 0] = run_r
            zlow[s, 1] = run_i
            zmin[s, 0] = cut_r
            zmin[s, 1] = cut_i
        ztot[zz, 0] = run_r
        ztot[zz, 1] = run_i
        for d in far:
            pltpu.make_async_remote_copy(
                src_ref=ztot.at[zz], dst_ref=ztot.at[zz], send_sem=zt_send, recv_sem=zt_recv,
                device_id=at_other(lax.rem(zz + d, slabs)), device_id_type=MESH,
            ).start()
    def trunk_z():
        wait_bytes(zt_recv, ztot.at[pl.ds(0, slabs - 1)])
        run_r = jnp.zeros((8, LANES), F32)
        run_i = run_r
        for z in range(slabs):
            zpre[z, 0] = run_r
            zpre[z, 1] = run_i
            run_r += ztot[z, 0]
            run_i += ztot[z, 1]

    def do(name):
        if name == "P":
            tables()
            for c in range(3, nodes):
                give(c).start()
        elif name == "S":
            slab_z()
        elif name == "Z":
            trunk_z()
        elif name == "X":
            open_up()
        elif name[0] == "G":
            give(int(name[1])).wait_recv()
            pass_on(int(name[1])).start()
        elif name[0] == "L":
            c = int(name[1])
            if c:
                pass_on(c).wait_recv()
            level(c)
        elif name[0] == "F":
            finish(int(name[1]))
        else:
            k, c = int(name[1]), int(name[2])
            if name[0] in "AC":
                currents(k, c, heads(k - 1, c) if k else None)
            if name[0] == "A":
                send_one(k, c)
            if name[0] == "M":
                products(k, c)
            if name[0] == "B":
                combine(k, c)

    for line in ORDER:
        for name in line.split():
            if int(name[-1] if name[-1].isdigit() else 0) < nodes:
                do(name)

    wait_bytes(zs_send, zsec.at[pl.ds(0, slab - 1)])
    wait_bytes(zt_send, ztot.at[pl.ds(0, slabs - 1)])
    for c in range(1, nodes):
        give(c).wait_send()
        pass_on(c).wait_send()
    for k in range(SWEEPS):
        for c in range(nodes):
            wait_bytes(one_send.at[k, c], one_sec.at[k, c, pl.ds(0, slab - 1)])
            wait_bytes(two_send.at[k, c], tiles(k, c, slabs - 1))


def store(in_r, in_i, out_r, out_i, sem):
    rows = in_r.shape[0] // PIECES
    copies = []
    for p in range(PIECES):
        where = pl.ds(p * rows, rows)
        copies.append(pltpu.make_async_copy(in_r.at[where], out_r.at[where], sem.at[0, p]))
        copies.append(pltpu.make_async_copy(in_i.at[where], out_i.at[where], sem.at[1, p]))
    for copy in copies:
        copy.start()
    for copy in copies:
        copy.wait()


def local(slabs, slab, nodes, factors, loadings, parents, load_base, lateral_z, trunk_z):
    chunk, depth = factors.shape
    scen = chunk * nodes
    width = loadings.shape[0]
    any_space = pl.BlockSpec(memory_space=pltpu.HBM)
    dma = pltpu.SemaphoreType.DMA
    hbm = functools.partial(pltpu.with_memory_space_constraint, memory_space=pltpu.HBM)
    out = jax.ShapeDtypeStruct((scen, width), F32)
    tile = (8, LANES)
    volts = pl.pallas_call(
        functools.partial(body, slabs, slab, nodes),
        out_shape=(out, out),
        in_specs=[any_space] * 6,
        out_specs=(pl.BlockSpec(memory_space=pltpu.VMEM),) * 2,
        scratch_shapes=[
            pltpu.VMEM((nodes, chunk, depth), BF16),
            pltpu.VMEM((nodes, width, chunk), F32),
            pltpu.VMEM((nodes, 4 * width, chunk), BF16),
            pltpu.VMEM((nodes, 2 * width, chunk), F32),
            pltpu.VMEM((nodes, chunk, 2 * width), F32),
            pltpu.VMEM((2 * width, 4 * width), BF16),
            pltpu.VMEM((2 * width, 2 * width), BF16),
            pltpu.VMEM((6 * width, 2 * width), BF16),
            pltpu.VMEM((width, LANES), F32),
            pltpu.VMEM((width, LANES), F32),
            pltpu.VMEM((SWEEPS, nodes, slab) + tile, F32),
            pltpu.VMEM((SWEEPS, nodes, slabs, 2) + tile, F32),
            pltpu.VMEM((SWEEPS, nodes, 2) + tile, F32),
            pltpu.VMEM((SWEEPS, nodes, 2) + tile, F32),
            pltpu.VMEM((slab, 2) + tile, F32),
            pltpu.VMEM((slab, 2) + tile, F32),
            pltpu.VMEM((slab, 2) + tile, F32),
            pltpu.VMEM((slabs, 2) + tile, F32),
            pltpu.VMEM((slabs, 2) + tile, F32),
            pltpu.VMEM((2, width, width), F32),
            pltpu.VMEM((width, depth), BF16),
            pltpu.VMEM((1, width), jnp.int32),
            pltpu.VMEM((2, width), F32),
            pltpu.VMEM((2, width), F32),
            pltpu.SMEM((2,), F32),
            dma((6,)),
            dma((nodes,)),
            dma((nodes,)),
            dma((nodes,)),
            dma((nodes,)),
            dma(()),
            dma(()),
            dma(()),
            dma(()),
            dma((SWEEPS, nodes)),
            dma((SWEEPS, nodes)),
            dma((SWEEPS, nodes)),
            dma((SWEEPS, nodes)),
        ],
        compiler_params=pltpu.CompilerParams(
            collective_id=0, has_side_effects=True, vmem_limit_bytes=48 * 1024 * 1024
        ),
    )(*[hbm(a) for a in (factors, loadings, parents.reshape(1, width), load_base, lateral_z, trunk_z.reshape(2))])
    return pl.pallas_call(
        store,
        out_shape=(out, out),
        in_specs=[pl.BlockSpec(memory_space=pltpu.VMEM)] * 2,
        out_specs=(any_space,) * 2,
        scratch_shapes=[dma((2, PIECES))],
        compiler_params=pltpu.CompilerParams(vmem_limit_bytes=1024 * 1024),
    )(*volts)


def solution(mesh):
    feeder = mesh.shape["feeder"]
    slab = 8 if feeder >= 64 else 2
    return jax.shard_map(
        functools.partial(local, feeder // slab, slab, mesh.shape["node"]),
        mesh=mesh,
        in_specs=(
            P("node", None),
            P(("feeder", "node"), None),
            P(("feeder", "node")),
            P(None, ("feeder", "node")),
            P(None, ("feeder", "node")),
            P(None, "feeder", "node"),
        ),
        out_specs=(P(None, ("feeder", "node")), P(None, ("feeder", "node"))),
        check_vma=False,
    )
```

```python
import functools

import jax
import jax.numpy as jnp
from jax import lax
from jax.experimental import pallas as pl
from jax.experimental.pallas import tpu as pltpu
from jax.sharding import PartitionSpec as P

MESH = pl.DeviceIdType.MESH
F32 = jnp.float32
BF16 = jnp.bfloat16
SWEEPS = 3
LANES = 128
ORDER = (
    "L0 C00 X P",
    "S B00",
    "G1 G2",
    "L1 A01",
    "L2 A02",
    "G3 M00 M01",
    "L3 A03",
    "M02 M03",
    "Z A10 B01",
    "B02 B03 M10 B10",
    "A11 A12 A13",
    "M11 M12 M13",
    "A20 B11 B12 B13",
    "M20 B20",
    "A21 A22 A23",
    "M21 M22 M23",
    "F0 B21 B22 B23",
    "F1 F2 F3",
)
PIECES = 4
PASS = 4


def dot(a, b, dims=((1,), (0,))):
    return lax.dot_general(a, b, (dims, ((), ())), preferred_element_type=F32)


def halves(value):
    high = value.astype(BF16)
    return high, (value - high.astype(F32)).astype(BF16)


def turn(tile):
    return pltpu.roll(tile, 4, 0)


def cmul(ratio, tile):
    return ratio[0] * tile + ratio[1] * turn(tile)


def body(
    slabs, slab, nodes, fac_ref, load_ref, par_ref, base_ref, latz_ref, trz_ref, out_r, out_i,
    fac, swing, cur, drop, dropl, wide, wlow, wlast, pcol, qcol, one_sec, two_sec, two_src, two_own,
    zsec, zlow, zmin, ztot, zpre, prep,
    load_v, par_v, base_v, latz_v, trz_s,
    local_sem, fac_send, fac_recv, pair_send, pair_recv, zs_send, zs_recv, zt_send, zt_recv,
    one_send, one_recv, two_send, two_recv,
):
    feeder = lax.axis_index("feeder")
    node = lax.axis_index("node")
    zz = feeder // slab
    ss = lax.rem(feeder, slab)
    core = lax.rem(feeder, 2)
    partner = feeder + 1 - 2 * core
    chunk = fac.shape[1]
    half = chunk // 2
    offsets = [0, 1, nodes - 1] + [o for o in range(2, nodes - 1)]

    def slab_mate(turn_):
        return lax.rem(ss + turn_, slab)

    def at_slab(mate):
        return {"feeder": zz * slab + mate, "node": node}

    def at_other(other):
        return {"feeder": other * slab + ss, "node": node}

    def at_node(offset):
        return {"feeder": feeder, "node": lax.rem(node + offset, nodes)}

    far = sorted(range(1, slabs), key=lambda d: -min(d, slabs - d))
    wide_turns = sorted(range(1, slab), key=lambda d: -min(d, slab - d))

    barrier = pltpu.get_barrier_semaphore()
    greeted = 0
    for d in far:
        pl.semaphore_signal(barrier, inc=1, device_id=at_other(lax.rem(zz + d, slabs)), device_id_type=MESH)
        greeted += 1
    for d in wide_turns:
        pl.semaphore_signal(barrier, inc=1, device_id=at_slab(slab_mate(d)), device_id_type=MESH)
        greeted += 1
    for o in offsets[1:]:
        pl.semaphore_signal(barrier, inc=1, device_id=at_node(o), device_id_type=MESH)
        greeted += 1

    copies = [
        pltpu.make_async_copy(fac_ref, fac.at[0], local_sem.at[0]),
        pltpu.make_async_copy(load_ref, load_v, local_sem.at[1]),
        pltpu.make_async_copy(base_ref, base_v, local_sem.at[2]),
        pltpu.make_async_copy(par_ref, par_v, local_sem.at[3]),
        pltpu.make_async_copy(latz_ref, latz_v, local_sem.at[4]),
        pltpu.make_async_copy(trz_ref, trz_s, local_sem.at[5]),
    ]
    for copy in copies:
        copy.start()
    for copy in copies:
        copy.wait()

    pcol[...] = jnp.broadcast_to(base_v[0:1, :], (LANES, LANES)).T
    qcol[...] = jnp.broadcast_to(base_v[1:2, :], (LANES, LANES)).T
    row8 = lax.broadcasted_iota(jnp.int32, (8, LANES), 0)
    upper = row8 < 4
    z_real = trz_s[0]
    z_imag = trz_s[1]
    zsec[ss, 0] = jnp.zeros((8, LANES), F32) + z_real
    zsec[ss, 1] = jnp.where(upper, -z_imag, z_imag)

    def level(c):
        for q in range(PASS):
            lo = q * LANES
            lev = dot(load_v[...], fac[c, lo:lo + LANES, :], ((1,), (1,)))
            swing[c, :, lo:lo + LANES] = 1.0 + 0.5 * jnp.tanh(lev.astype(BF16).astype(F32))

    rows = 16

    def currents(k, c, head):
        for q in range(PASS):
            lo = q * LANES
            if k:
                head_r = jnp.broadcast_to(head[q:q + 1, :], (rows, LANES))
                head_i = jnp.broadcast_to(head[q + 4:q + 5, :], (rows, LANES))

            def step(i, sums):
                at = pl.multiple_of(i * rows, rows)
                sw = swing[c, pl.ds(at, rows), lo:lo + LANES]
                p = pcol[pl.ds(at, rows), :]
                r = qcol[pl.ds(at, rows), :]
                if k:
                    vr = head_r - drop[c, pl.ds(at, rows), lo:lo + LANES]
                    vi = head_i - drop[c, pl.ds(LANES + at, rows), lo:lo + LANES]
                    t = sw / (vr * vr + vi * vi)
                    cr = t * (p * vr + r * vi)
                    ci = t * (p * vi - r * vr)
                else:
                    cr = sw * p
                    ci = -(sw * r)
                for part, value in ((0, cr), (1, ci)):
                    high, low = halves(value)
                    cur[c, pl.ds(part * LANES + at, rows), lo:lo + LANES] = high
                    cur[c, pl.ds((part + 2) * LANES + at, rows), lo:lo + LANES] = low
                return (
                    sums[0] + cr[0:8] + cr[8:16],
                    sums[1] + ci[0:8] + ci[8:16],
                )

            zero = jnp.zeros((8, LANES), F32)
            sum_r, sum_i = lax.fori_loop(0, LANES // rows, step, (zero, zero), unroll=8)
            one_sec[k, c, ss, q:q + 1, :] = jnp.sum(sum_r, axis=0, keepdims=True)
            one_sec[k, c, ss, q + 4:q + 5, :] = jnp.sum(sum_i, axis=0, keepdims=True)

    def send_one(k, c):
        for d in wide_turns:
            mate = slab_mate(d)
            pltpu.make_async_remote_copy(
                src_ref=one_sec.at[k, c, ss], dst_ref=one_sec.at[k, c, ss],
                send_sem=one_send.at[k, c], recv_sem=one_recv.at[k, c],
                device_id=at_slab(mate), device_id_type=MESH,
            ).start()

    def wait_bytes(sem, block):
        pltpu.make_async_copy(block, block, sem).wait()

    def combine(k, c):
        wait_bytes(one_recv.at[k, c], one_sec.at[k, c, pl.ds(0, slab - 1)])
        total = jnp.zeros((8, LANES), F32)
        weighted = total
        own = total
        for s in range(slab):
            tile = one_sec[k, c, s]
            swapped = turn(tile)
            total += tile
            weighted += zlow[s, 0] * tile + zlow[s, 1] * swapped
            own += zmin[s, 0] * tile + zmin[s, 1] * swapped
        if k or c:
            shift = cmul((zpre[zz, 0], zpre[zz, 1]), total)
            weighted += shift
            own += shift
        two_src[k, c, 0] = total
        two_src[k, c, 1] = weighted
        two_own[k, c, 0] = total
        two_own[k, c, 1] = own
        for d in far:
            other = lax.rem(zz + d, slabs)
            if k or c:
                later = (other > zz).astype(jnp.int32)
                source = two_src.at[k, c, pl.ds(later, 1)]
                target = two_sec.at[k, c, zz, pl.ds(0, 1)]
            else:
                source = two_src.at[k, c]
                target = two_sec.at[k, c, zz]
            pltpu.make_async_remote_copy(
                src_ref=source, dst_ref=target,
                send_sem=two_send.at[k, c], recv_sem=two_recv.at[k, c],
                device_id=at_other(other), device_id_type=MESH,
            ).start()

    def tiles(k, c, count):
        if k or c:
            return two_sec.at[k, c, pl.ds(0, count), pl.ds(0, 1)]
        return two_sec.at[k, c, pl.ds(0, count)]

    def heads(k, c):
        wait_bytes(two_recv.at[k, c], tiles(k, c, slabs - 1))
        near = two_own[k, c, 1]
        beyond = jnp.zeros((8, LANES), F32)
        if not (k or c):
            near += cmul((zpre[zz, 0], zpre[zz, 1]), two_own[k, c, 0])
        for z in range(slabs):
            tile = two_sec[k, c, z, 0]
            beyond += jnp.where(z > zz, tile, 0.0)
            if k or c:
                near += jnp.where(z < zz, tile, 0.0)
            else:
                given = cmul((zpre[z, 0], zpre[z, 1]), tile) + two_sec[k, c, z, 1]
                near += jnp.where(z < zz, given, 0.0)
        here = (zpre[zz, 0] + zlow[ss, 0], zpre[zz, 1] + zlow[ss, 1])
        return jnp.where(upper, 1.0, 0.0) - near - cmul(here, beyond)

    def products(k, c):
        if k < SWEEPS - 1:
            drop[c] = dot(wide[...], cur[c]) + dot(wlow[...], cur[c, 0:2 * LANES, :])
        else:
            dropl[c] = dot(cur[c], wlast[0:4 * LANES, :], ((0,), (0,))) + dot(
                cur[c, 0:2 * LANES, :], wlast[4 * LANES:6 * LANES, :], ((0,), (0,))
            )

    def finish(c):
        head = heads(SWEEPS - 1, c).T
        at = lax.rem(node + offsets[c], nodes) * chunk
        for q in range(PASS):
            where = pl.ds(pl.multiple_of(at + q * LANES, LANES), LANES)
            lo = q * LANES
            out_r[where, :] = head[:, q:q + 1] - dropl[c, lo:lo + LANES, 0:LANES]
            out_i[where, :] = head[:, q + 4:q + 5] - dropl[c, lo:lo + LANES, LANES:2 * LANES]

    mine = pl.ds(pl.multiple_of(core * half, half), half)

    def give(c):
        return pltpu.make_async_remote_copy(
            src_ref=fac.at[0, mine], dst_ref=fac.at[c, mine],
            send_sem=fac_send.at[c], recv_sem=fac_recv.at[c],
            device_id=at_node(nodes - offsets[c]), device_id_type=MESH,
        )

    def pass_on(c):
        return pltpu.make_async_remote_copy(
            src_ref=fac.at[c, mine], dst_ref=fac.at[c, mine],
            send_sem=pair_send.at[c], recv_sem=pair_recv.at[c],
            device_id={"feeder": partner, "node": node}, device_id_type=MESH,
        )

    def open_up():
        pl.semaphore_wait(barrier, greeted)
        for d in wide_turns:
            pltpu.make_async_remote_copy(
                src_ref=zsec.at[ss], dst_ref=zsec.at[ss], send_sem=zs_send, recv_sem=zs_recv,
                device_id=at_slab(slab_mate(d)), device_id_type=MESH,
            ).start()
        send_one(0, 0)
        for c in range(1, min(nodes, 3)):
            give(c).start()

    def tables():
        width = LANES
        down = lax.broadcasted_iota(jnp.int32, (width, width), 0)
        across = lax.broadcasted_iota(jnp.int32, (width, width), 1)
        adjacent = jnp.where(jnp.broadcast_to(par_v[...], (width, width)) == down, 1.0, 0.0).T
        paths = jnp.where(down == across, 1.0, 0.0) + adjacent
        power = adjacent.astype(BF16)
        for turn_ in range((width - 1).bit_length() - 1):
            power = dot(power, power).astype(BF16)
            paths = paths + dot(paths.astype(BF16), power)
        paths_low = paths.astype(BF16)
        for part in range(2):
            z_row = jnp.broadcast_to(latz_v[part:part + 1, :], (width, width))
            z_high, z_mid = halves(z_row)
            z_low = (z_row - z_high.astype(F32) - z_mid.astype(F32)).astype(BF16)
            table = jnp.zeros((width, width), F32)
            for piece in (z_low, z_mid, z_high):
                table += dot((paths * piece.astype(F32)).astype(BF16), paths_low, ((1,), (1,)))
            prep[part] = table
        for part, sign, r0, c0 in ((0, 1.0, 0, 0), (1, -1.0, 0, 1), (1, 1.0, 1, 0), (0, 1.0, 1, 1)):
            high, low = halves(prep[part] * sign)
            rs, cs = slice(r0 * width, (r0 + 1) * width), slice(c0 * width, (c0 + 1) * width)
            wide[rs, cs] = high
            wide[rs, (c0 + 2) * width:(c0 + 3) * width] = high
            wlow[rs, cs] = low
            ts, us = slice(c0 * width, (c0 + 1) * width), slice(r0 * width, (r0 + 1) * width)
            wlast[ts, us] = high
            wlast[(c0 + 2) * width:(c0 + 3) * width, us] = high
            wlast[(c0 + 4) * width:(c0 + 5) * width, us] = low

    def slab_z():
        wait_bytes(zs_recv, zsec.at[pl.ds(0, slab - 1)])
        run_r = jnp.zeros((8, LANES), F32)
        run_i = run_r
        cut_r = run_r
        cut_i = run_r
        for s in range(slab):
            run_r += zsec[s, 0]
            run_i += zsec[s, 1]
            cut_r += jnp.where(s <= ss, zsec[s, 0], 0.0)
            cut_i += jnp.where(s <= ss, zsec[s, 1], 0.0)
            zlow[s, 0] = run_r
            zlow[s, 1] = run_i
            zmin[s, 0] = cut_r
            zmin[s, 1] = cut_i
        ztot[zz, 0] = run_r
        ztot[zz, 1] = run_i
        for d in far:
            pltpu.make_async_remote_copy(
                src_ref=ztot.at[zz], dst_ref=ztot.at[zz], send_sem=zt_send, recv_sem=zt_recv,
                device_id=at_other(lax.rem(zz + d, slabs)), device_id_type=MESH,
            ).start()
    def trunk_z():
        wait_bytes(zt_recv, ztot.at[pl.ds(0, slabs - 1)])
        run_r = jnp.zeros((8, LANES), F32)
        run_i = run_r
        for z in range(slabs):
            zpre[z, 0] = run_r
            zpre[z, 1] = run_i
            run_r += ztot[z, 0]
            run_i += ztot[z, 1]

    def do(name):
        if name == "P":
            tables()
            for c in range(3, nodes):
                give(c).start()
        elif name == "S":
            slab_z()
        elif name == "Z":
            trunk_z()
        elif name == "X":
            open_up()
        elif name[0] == "G":
            give(int(name[1])).wait_recv()
            pass_on(int(name[1])).start()
        elif name[0] == "L":
            c = int(name[1])
            if c:
                pass_on(c).wait_recv()
            level(c)
        elif name[0] == "F":
            finish(int(name[1]))
        else:
            k, c = int(name[1]), int(name[2])
            if name[0] in "AC":
                currents(k, c, heads(k - 1, c) if k else None)
            if name[0] == "A":
                send_one(k, c)
            if name[0] == "M":
                products(k, c)
            if name[0] == "B":
                combine(k, c)

    for line in ORDER:
        for name in line.split():
            if int(name[-1] if name[-1].isdigit() else 0) < nodes:
                do(name)

    wait_bytes(zs_send, zsec.at[pl.ds(0, slab - 1)])
    wait_bytes(zt_send, ztot.at[pl.ds(0, slabs - 1)])
    for c in range(1, nodes):
        give(c).wait_send()
        pass_on(c).wait_send()
    for k in range(SWEEPS):
        for c in range(nodes):
            wait_bytes(one_send.at[k, c], one_sec.at[k, c, pl.ds(0, slab - 1)])
            wait_bytes(two_send.at[k, c], tiles(k, c, slabs - 1))


def store(in_r, in_i, out_r, out_i, sem):
    rows = in_r.shape[0] // PIECES
    copies = []
    for p in range(PIECES):
        where = pl.ds(p * rows, rows)
        copies.append(pltpu.make_async_copy(in_r.at[where], out_r.at[where], sem.at[0, p]))
        copies.append(pltpu.make_async_copy(in_i.at[where], out_i.at[where], sem.at[1, p]))
    for copy in copies:
        copy.start()
    for copy in copies:
        copy.wait()


def local(slabs, slab, nodes, factors, loadings, parents, load_base, lateral_z, trunk_z):
    chunk, depth = factors.shape
    scen = chunk * nodes
    width = loadings.shape[0]
    any_space = pl.BlockSpec(memory_space=pltpu.HBM)
    dma = pltpu.SemaphoreType.DMA
    hbm = functools.partial(pltpu.with_memory_space_constraint, memory_space=pltpu.HBM)
    out = jax.ShapeDtypeStruct((scen, width), F32)
    tile = (8, LANES)
    volts = pl.pallas_call(
        functools.partial(body, slabs, slab, nodes),
        out_shape=(out, out),
        in_specs=[any_space] * 6,
        out_specs=(pl.BlockSpec(memory_space=pltpu.VMEM),) * 2,
        scratch_shapes=[
            pltpu.VMEM((nodes, chunk, depth), BF16),
            pltpu.VMEM((nodes, width, chunk), F32),
            pltpu.VMEM((nodes, 4 * width, chunk), BF16),
            pltpu.VMEM((nodes, 2 * width, chunk), F32),
            pltpu.VMEM((nodes, chunk, 2 * width), F32),
            pltpu.VMEM((2 * width, 4 * width), BF16),
            pltpu.VMEM((2 * width, 2 * width), BF16),
            pltpu.VMEM((6 * width, 2 * width), BF16),
            pltpu.VMEM((width, LANES), F32),
            pltpu.VMEM((width, LANES), F32),
            pltpu.VMEM((SWEEPS, nodes, slab) + tile, F32),
            pltpu.VMEM((SWEEPS, nodes, slabs, 2) + tile, F32),
            pltpu.VMEM((SWEEPS, nodes, 2) + tile, F32),
            pltpu.VMEM((SWEEPS, nodes, 2) + tile, F32),
            pltpu.VMEM((slab, 2) + tile, F32),
            pltpu.VMEM((slab, 2) + tile, F32),
            pltpu.VMEM((slab, 2) + tile, F32),
            pltpu.VMEM((slabs, 2) + tile, F32),
            pltpu.VMEM((slabs, 2) + tile, F32),
            pltpu.VMEM((2, width, width), F32),
            pltpu.VMEM((width, depth), BF16),
            pltpu.VMEM((1, width), jnp.int32),
            pltpu.VMEM((2, width), F32),
            pltpu.VMEM((2, width), F32),
            pltpu.SMEM((2,), F32),
            dma((6,)),
            dma((nodes,)),
            dma((nodes,)),
            dma((nodes,)),
            dma((nodes,)),
            dma(()),
            dma(()),
            dma(()),
            dma(()),
            dma((SWEEPS, nodes)),
            dma((SWEEPS, nodes)),
            dma((SWEEPS, nodes)),
            dma((SWEEPS, nodes)),
        ],
        compiler_params=pltpu.CompilerParams(
            collective_id=0, has_side_effects=True, vmem_limit_bytes=48 * 1024 * 1024
        ),
    )(*[hbm(a) for a in (factors, loadings, parents.reshape(1, width), load_base, lateral_z, trunk_z.reshape(2))])
    return pl.pallas_call(
        store,
        out_shape=(out, out),
        in_specs=[pl.BlockSpec(memory_space=pltpu.VMEM)] * 2,
        out_specs=(any_space,) * 2,
        scratch_shapes=[dma((2, PIECES))],
        compiler_params=pltpu.CompilerParams(vmem_limit_bytes=1024 * 1024),
    )(*volts)


def solution(mesh):
    feeder = mesh.shape["feeder"]
    slab = 8 if feeder >= 64 else 2
    return jax.shard_map(
        functools.partial(local, feeder // slab, slab, mesh.shape["node"]),
        mesh=mesh,
        in_specs=(
            P("node", None),
            P(("feeder", "node"), None),
            P(("feeder", "node")),
            P(None, ("feeder", "node")),
            P(None, ("feeder", "node")),
            P(None, "feeder", "node"),
        ),
        out_specs=(P(None, ("feeder", "node")), P(None, ("feeder", "node"))),
        check_vma=False,
    )
```
